512 devices in a mesh: gx: 32 (over z_lo, y, core), gy: 16 (over z_hi, x).
Axes of the slice: x: 4, y: 4, z: 16 (z_hi: 4, z_lo: 4; z = z_hi * 4 + z_lo), core: 2. Of those that a mesh axis runs over, the one named last changes fastest.
Arguments:
- current: bfloat16 [4, 256, 256, 128], P(None, 'gx', 'gy'), may hold values from -6 to 6
- previous: bfloat16 [4, 256, 256, 128], P(None, 'gx', 'gy'), may hold values from -6 to 6
- offsets: int32 [4, 2], replicated, may hold values from -6 to 6, as said below
- center_rows: int32 [4, 64], replicated, may hold values from 0 to 255
- center_cols: int32 [4, 64], replicated, may hold values from 0 to 255
- classes: int32 [4, 64], replicated, may hold values from 0 to 9
- w_merge1: bfloat16 [3, 3, 256, 128], replicated, may hold values from -0.125 to 0.125
- w_merge2: bfloat16 [3, 3, 128, 128], replicated, may hold values from -0.1875 to 0.1875
- w_head: bfloat16 [128, 10], replicated, may hold values from -0.5 to 0.5
Outputs:
- loss: float32 [], replicated
- grad_merge1: float32 [3, 3, 256, 128], replicated
- grad_merge2: float32 [3, 3, 128, 128], replicated
- grad_head: float32 [128, 10], replicated
- grad_current: bfloat16 [4, 256, 256, 128], P(None, 'gx', 'gy')
- grad_previous: bfloat16 [4, 256, 256, 128], P(None, 'gx', 'gy')
The draws below stay inside these ranges and needn't reach their ends.
Inputs may be any that keep to these rules, and one draw needn't show every extreme that they name: `offsets`: no offset is zero; along each of the two axes half of the scenes have a positive offset and half a negative one; in every draw some offset has magnitude exactly 6.
All inputs are finite; a program needn't handle non-finite values.
Results may differ from the reference program's by a relative error of at most 0.0085.
Values may be sent and summed in bfloat16 or wider, within the bound.
A program may use at most 64 MiB of HBM per device.

```python
import jax
import jax.numpy as jnp
from jax import lax

CH = 128
CLS = 10
SCENES = 4
OBJ = 64
R_DEV = 8
C_DEV = 16
SHIFT = 6
NX = 256
NY = 256


def draw_offsets(key, part):
    base = jax.random.fold_in(key, 23)
    keys = jax.random.split(base, 5)
    perm_rows = jax.random.permutation(keys[0], SCENES)
    perm_cols = jax.random.permutation(keys[1], SCENES)
    signs = jnp.stack([jnp.where(perm_rows < SCENES // 2, 1, -1), jnp.where(perm_cols < SCENES // 2, 1, -1)], axis=1)
    sizes = jax.random.randint(keys[2], (SCENES, 2), 1, SHIFT + 1)
    scene_pick = jax.random.randint(keys[3], (), 0, SCENES)
    axis_pick = jax.random.randint(keys[4], (), 0, 2)
    chosen = (jnp.arange(SCENES)[:, None] == scene_pick) & (jnp.arange(2)[None, :] == axis_pick)
    sizes = jnp.where(chosen, SHIFT, sizes)
    return (signs * sizes).astype(jnp.int32)


def center_cells(key):
    base = jax.random.fold_in(key, 41)
    keys = jax.random.split(base, 6)
    tile_row = jax.random.randint(keys[0], (), 0, NX // R_DEV)
    tile_col = jax.random.randint(keys[1], (), 0, NY // C_DEV)
    spread_rows = jax.random.randint(keys[2], (SCENES, OBJ), 0, NX)
    spread_cols = jax.random.randint(keys[3], (SCENES, OBJ), 0, NY)
    local_rows = jax.random.randint(keys[4], (SCENES, OBJ), 0, R_DEV)
    local_cols = jax.random.randint(keys[5], (SCENES, OBJ), 0, C_DEV)
    near = jnp.arange(OBJ)[None, :] < OBJ // 4
    rows_out = jnp.where(near, tile_row * R_DEV + local_rows, spread_rows)
    cols_out = jnp.where(near, tile_col * C_DEV + local_cols, spread_cols)
    return (rows_out.astype(jnp.int32), cols_out.astype(jnp.int32))


def draw_center_rows(key, part):
    return center_cells(key)[0]


def draw_center_cols(key, part):
    return center_cells(key)[1]


def place_ends(drawn, key, smallest, top_value):
    extent = drawn.shape
    index_at = [jax.random.randint(jax.random.fold_in(key, axis), (), 0, extent[axis]) for axis in range(len(extent))]
    drawn = drawn.at[tuple(index_at)].set(smallest)
    longest = extent.index(max(extent))
    index_at[longest] = (index_at[longest] + 1) % extent[longest]
    return drawn.at[tuple(index_at)].set(top_value)


def level_of(stream_key, dims, shards, smallest, top_value):
    loudness = 1.0
    for dim, shards_of in shards:
        heights = jax.random.uniform(jax.random.fold_in(jax.random.fold_in(stream_key, 6), dim), (shards_of,), jnp.float32, smallest / len(shards), top_value / len(shards))
        loudness = loudness * jnp.repeat(jnp.exp(heights), dims[dim] // shards_of).reshape((-1,) + (1,) * (len(dims) - 1 - dim))
    return loudness


def gaussian(stream_key, shape, spread, bound, shards=(), kind=jnp.bfloat16):
    result = jax.random.normal(stream_key, shape, jnp.float32) * spread
    if len(shards) > 0:
        result = level_of(stream_key, shape, shards, -0.22, 0.18) * result
    return jnp.clip(result, min=-bound, max=bound).astype(kind)


def setup_inputs(seed: int = 0) -> dict:
    key_list = jax.random.split(jax.random.key(seed), 10)
    current = gaussian(key_list[0], (SCENES, NX, NY, CH), 1.0, 6.0, ((1, 32), (2, 16)))
    previous = gaussian(key_list[1], (SCENES, NX, NY, CH), 1.0, 6.0, ((1, 32), (2, 16)))
    offsets = draw_offsets(jax.random.fold_in(key_list[9], 71), 0)
    center_rows = draw_center_rows(jax.random.fold_in(key_list[9], 71), 0)
    center_cols = draw_center_cols(jax.random.fold_in(key_list[9], 71), 0)
    classes = place_ends(jax.random.randint(key_list[5], (SCENES, OBJ), 0, CLS), jax.random.fold_in(key_list[5], 1), 0, CLS - 1).astype(jnp.int32)
    w_merge1 = gaussian(key_list[6], (3, 3, 2 * CH, CH), (18 * CH) ** -0.5, 0.125)
    w_merge2 = gaussian(key_list[7], (3, 3, CH, CH), (9 * CH) ** -0.5, 0.1875)
    w_head = gaussian(key_list[8], (CH, CLS), CH ** -0.5, 0.5)
    return dict(current=current, previous=previous, offsets=offsets, center_rows=center_rows, center_cols=center_cols, classes=classes, w_merge1=w_merge1, w_merge2=w_merge2, w_head=w_head)


def silu_grad(value):
    sig = jax.nn.sigmoid(value)
    return sig * (1.0 + value * (1.0 - sig))

def convolve(padded, weight, rows, cols):
    total = jnp.zeros((padded.shape[0] * rows * cols, weight.shape[3]), jnp.float32)
    for i in range(3):
        for j in range(3):
            window = padded[:, i:i + rows, j:j + cols].reshape(-1, padded.shape[3])
            total = total + jnp.dot(window, weight[i, j], preferred_element_type=jnp.float32)
    return total

def back_convolve(padded, weight, rows, cols):
    total = jnp.zeros((padded.shape[0] * rows * cols, weight.shape[2]), jnp.float32)
    for i in range(3):
        for j in range(3):
            window = padded[:, 2 - i:2 - i + rows, 2 - j:2 - j + cols].reshape(-1, padded.shape[3])
            total = total + jnp.dot(window, weight[i, j].T, preferred_element_type=jnp.float32)
    return total

def weight_grad(padded, upstream, rows, cols):
    taps = []
    for i in range(3):
        for j in range(3):
            window = padded[:, i:i + rows, j:j + cols].reshape(-1, padded.shape[3])
            taps.append(lax.dot_general(window, upstream, (((0,), (0,)), ((), ())), preferred_element_type=jnp.float32))
    return jnp.stack(taps).reshape(3, 3, padded.shape[3], upstream.shape[1])

def focal(logits, target, positive, count):
    prob = jax.nn.sigmoid(logits)
    log_p = jax.nn.log_sigmoid(logits)
    log_q = jax.nn.log_sigmoid(-logits)
    miss = 1.0 - target
    miss = miss * miss
    pos_term = -(1.0 - prob) * (1.0 - prob) * log_p
    neg_term = -(miss * miss) * prob * prob * log_q
    return jnp.sum(jnp.where(positive, pos_term, neg_term)) / count

def pad_cells(field, width):
    return jnp.pad(field, ((0, 0), (width, width), (width, width), (0, 0)))

def scene_target(rows_c, cols_c, cls):
    onehot = (cls[:, None] == jnp.arange(CLS, dtype=jnp.int32)[None, :]).astype(jnp.float32)
    col_ids = jnp.arange(NY, dtype=jnp.int32)
    dc = (col_ids[:, None] - cols_c[None, :]).astype(jnp.float32)

    def one_row(row):
        dr = (row - rows_c).astype(jnp.float32)
        bump = jnp.exp(-(dr * dr)[None, :] / 8.0 - dc * dc / 8.0)
        tgt = lax.optimization_barrier(jnp.max(bump[:, :, None] * onehot[None, :, :], axis=1))
        hit = ((row == rows_c)[None, :] & (col_ids[:, None] == cols_c[None, :])).astype(jnp.float32)
        pos = jnp.dot(hit, onehot) > 0.5
        return (tgt, pos)
    return lax.map(one_row, jnp.arange(NX, dtype=jnp.int32))

def reference(current, previous, offsets, center_rows, center_cols, classes, w_merge1, w_merge2, w_head):
    chans = current.shape[3]
    scenes = current.shape[0]

    def move(wide, offset, sign):
        zero = jnp.zeros((), jnp.int32)
        start_r = (SHIFT + sign * offset[0]).astype(jnp.int32)
        start_c = (SHIFT + sign * offset[1]).astype(jnp.int32)
        return lax.dynamic_slice(wide, (start_r, start_c, zero), (NX, NY, chans))
    aligned = jax.vmap(lambda w, o: move(w, o, -1))(pad_cells(previous, SHIFT), offsets)
    stacked = jnp.concatenate([current, aligned], axis=3)
    stack_pad = pad_cells(stacked, 1)
    pre1 = convolve(stack_pad, w_merge1, NX, NY)
    hidden1 = jax.nn.silu(pre1).astype(jnp.bfloat16).reshape(scenes, NX, NY, chans)
    hid_pad = pad_cells(hidden1, 1)
    pre2 = convolve(hid_pad, w_merge2, NX, NY)
    hidden2 = jax.nn.silu(pre2).astype(jnp.bfloat16)
    logits = (jnp.dot(hidden2, w_head, preferred_element_type=jnp.float32) - 2.19).reshape(scenes, NX, NY, CLS)
    target, positive = jax.vmap(scene_target)(center_rows, center_cols, classes)
    loss, back = jax.vjp(lambda z: focal(z, target, positive, SCENES * OBJ), logits)
    d_logits = back(jnp.ones((), jnp.float32))[0].astype(jnp.bfloat16).reshape(-1, CLS)
    grad_head = lax.dot_general(hidden2, d_logits, (((0,), (0,)), ((), ())), preferred_element_type=jnp.float32)
    d_hid2 = jnp.dot(d_logits, w_head.T, preferred_element_type=jnp.float32)
    d_pre2 = (d_hid2 * silu_grad(pre2)).astype(jnp.bfloat16)
    grad_merge2 = weight_grad(hid_pad, d_pre2, NX, NY)
    dpad2 = pad_cells(d_pre2.reshape(scenes, NX, NY, chans), 1)
    d_hid1 = back_convolve(dpad2, w_merge2, NX, NY)
    d_pre1 = (d_hid1 * silu_grad(pre1)).astype(jnp.bfloat16)
    grad_merge1 = weight_grad(stack_pad, d_pre1, NX, NY)
    dpad1 = pad_cells(d_pre1.reshape(scenes, NX, NY, chans), 1)
    d_stack = back_convolve(dpad1, w_merge1, NX, NY).reshape(scenes, NX, NY, 2 * chans)
    grad_current = d_stack[..., :chans].astype(jnp.bfloat16)
    d_aligned = d_stack[..., chans:].astype(jnp.bfloat16)
    grad_previous = jax.vmap(lambda w, o: move(w, o, 1))(pad_cells(d_aligned, SHIFT), offsets)
    return (loss, grad_merge1, grad_merge2, grad_head, grad_current, grad_previous)
```

```python
import jax
import jax.numpy as jnp
from jax import lax
from jax.experimental import pallas as pl
from jax.experimental.pallas import tpu as pltpu
from jax.sharding import PartitionSpec as P


ROWS = 4096
HALF, QX, QY, QZ = ROWS // 2, ROWS // 8, ROWS // 32, ROWS // 512
MESH = pl.DeviceIdType.MESH


def place():
    gx, gy = lax.axis_index("gx"), lax.axis_index("gy")
    return gx % 2, gy % 4, (gx // 2) % 4, (gy // 4) * 4 + gx // 8


def device(core, x, y, z):
    return {"gx": ((z % 4) * 4 + y) * 2 + core, "gy": (z // 4) * 4 + x}


def reduce_kernel(
    part_ref, out_ref,
    half_in, half, x_out, x_in, x_own, y_out, y_in, y_own, z_in, z_all,
    y_all, x_all, c_all, c_send, c_recv, x_send, x_recv, y_send, y_recv, z_send, z_recv,
):
    core, x, y, z = place()
    partner = device(1 - core, x, y, z)
    xs = [device(core, (x + d) % 4, y, z) for d in range(1, 4)]
    ys = [device(core, x, (y + d) % 4, z) for d in range(1, 4)]
    zs = [device(core, x, y, (z + d) % 16) for d in range(1, 16)]
    barrier = pltpu.get_barrier_semaphore()
    for peer in [partner, *xs, *ys, *zs]:
        pl.semaphore_signal(barrier, inc=1, device_id=peer, device_id_type=MESH)
    pl.semaphore_wait(barrier, 22)

    def copy(src, dst, send, recv, peer):
        one = pltpu.make_async_remote_copy(
            src_ref=src, dst_ref=dst, send_sem=send, recv_sem=recv,
            device_id=peer, device_id_type=MESH,
        )
        one.start()
        return one

    theirs = pl.multiple_of((1 - core) * HALF, HALF)
    mine = pl.multiple_of(core * HALF, HALF)
    c = copy(part_ref.at[pl.ds(theirs, HALF)], half_in, c_send.at[0], c_recv.at[0], partner)
    c.wait()
    total = part_ref[pl.ds(mine, HALF)] + half_in[...]
    half[...] = total
    x_out[...] = total.astype(jnp.bfloat16)
    cs = [
        copy(x_out.at[pl.ds(pl.multiple_of(((x + d) % 4) * QX, QX), QX)], x_in.at[d - 1],
             x_send.at[d - 1], x_recv.at[d - 1], xs[d - 1])
        for d in range(1, 4)
    ]
    total = half[pl.ds(pl.multiple_of(x * QX, QX), QX)]
    for d in range(3):
        cs[d].wait()
        total = total + x_in[d].astype(jnp.float32)
    x_own[...] = total
    y_out[...] = total.astype(jnp.bfloat16)
    cs = [
        copy(y_out.at[pl.ds(pl.multiple_of(((y + d) % 4) * QY, QY), QY)], y_in.at[d - 1],
             y_send.at[d - 1], y_recv.at[d - 1], ys[d - 1])
        for d in range(1, 4)
    ]
    total = x_own[pl.ds(pl.multiple_of(y * QY, QY), QY)]
    for d in range(3):
        cs[d].wait()
        total = total + y_in[d].astype(jnp.float32)
    y_own[...] = total
    cs = [
        copy(y_own.at[pl.ds(pl.multiple_of(((z + d) % 16) * QZ, QZ), QZ)], z_in.at[d - 1],
             z_send.at[d - 1], z_recv.at[d - 1], zs[d - 1])
        for d in range(1, 16)
    ]
    total = y_own[pl.ds(pl.multiple_of(z * QZ, QZ), QZ)]
    for d in range(15):
        cs[d].wait()
        total = total + z_in[d]
    own = pl.ds(pl.multiple_of(z * QZ, QZ), QZ)
    z_all[own] = total
    cs = [
        copy(z_all.at[own], z_all.at[own], z_send.at[14 + d], z_recv.at[14 + d], zs[d - 1])
        for d in range(1, 16)
    ]
    for one in cs:
        one.wait()
    own = pl.ds(pl.multiple_of(y * QY, QY), QY)
    y_all[own] = z_all[...].astype(jnp.bfloat16)
    cs = [
        copy(y_all.at[own], y_all.at[own], y_send.at[2 + d], y_recv.at[2 + d], ys[d - 1])
        for d in range(1, 4)
    ]
    for one in cs:
        one.wait()
    own = pl.ds(pl.multiple_of(x * QX, QX), QX)
    x_all[own] = y_all[...]
    cs = [
        copy(x_all.at[own], x_all.at[own], x_send.at[2 + d], x_recv.at[2 + d], xs[d - 1])
        for d in range(1, 4)
    ]
    for one in cs:
        one.wait()
    c = copy(x_all, c_all, c_send.at[1], c_recv.at[1], partner)
    out_ref[pl.ds(mine, HALF)] = x_all[...].astype(jnp.float32)
    c.wait()
    out_ref[pl.ds(theirs, HALF)] = c_all[...].astype(jnp.float32)


def all_reduce(part):
    bf, f = jnp.bfloat16, jnp.float32
    V, D = pltpu.VMEM, pltpu.SemaphoreType.DMA
    return pl.pallas_call(
        reduce_kernel,
        out_shape=jax.ShapeDtypeStruct((ROWS, 128), f),
        in_specs=[pl.BlockSpec(memory_space=pltpu.VMEM)],
        out_specs=pl.BlockSpec(memory_space=pltpu.VMEM),
        scratch_shapes=[
            V((HALF, 128), f), V((HALF, 128), f), V((HALF, 128), bf), V((3, QX, 128), bf), V((QX, 128), f),
            V((QX, 128), bf), V((3, QY, 128), bf), V((QY, 128), f), V((15, QZ, 128), f), V((QY, 128), f),
            V((QX, 128), bf), V((HALF, 128), bf), V((HALF, 128), bf),
            D((2,)), D((2,)), D((6,)), D((6,)), D((6,)), D((6,)), D((30,)), D((30,)),
        ],
        compiler_params=pltpu.CompilerParams(collective_id=1, has_side_effects=True),
        name="all_reduce",
    )(part)


def extended(block, sides, width):
    for axis, dim in sides:
        count = lax.axis_size(axis)
        forward = [(i, i + 1) for i in range(count - 1)]
        backward = [(target, source) for source, target in forward]
        low = lax.ppermute(
            lax.slice_in_dim(block, block.shape[dim] - width, None, axis=dim), axis, forward
        )
        high = lax.ppermute(lax.slice_in_dim(block, 0, width, axis=dim), axis, backward)
        block = jnp.concatenate([low, block, high], axis=dim)
    return block


def silu_grad(value):
    sig = jax.nn.sigmoid(value)
    return sig * (1.0 + value * (1.0 - sig))


def convolve(padded, weight, rows, cols):
    total = jnp.zeros((padded.shape[0] * rows * cols, weight.shape[3]), jnp.float32)
    for i in range(3):
        for j in range(3):
            window = padded[:, i : i + rows, j : j + cols].reshape(-1, padded.shape[3])
            total = total + jnp.dot(window, weight[i, j], preferred_element_type=jnp.float32)
    return total


def back_convolve(padded, weight, rows, cols):
    total = jnp.zeros((padded.shape[0] * rows * cols, weight.shape[2]), jnp.float32)
    for i in range(3):
        for j in range(3):
            window = padded[:, 2 - i : 2 - i + rows, 2 - j : 2 - j + cols].reshape(
                -1, padded.shape[3]
            )
            total = total + jnp.dot(window, weight[i, j].T, preferred_element_type=jnp.float32)
    return total


def weight_grad(padded, upstream, rows, cols):
    taps = []
    for i in range(3):
        for j in range(3):
            window = padded[:, i : i + rows, j : j + cols].reshape(-1, padded.shape[3])
            taps.append(
                lax.dot_general(
                    window, upstream, (((0,), (0,)), ((), ())), preferred_element_type=jnp.float32
                )
            )
    return jnp.stack(taps).reshape(3, 3, padded.shape[3], upstream.shape[1])


def focal(logits, target, positive, count):
    prob = jax.nn.sigmoid(logits)
    log_p = jax.nn.log_sigmoid(logits)
    log_q = jax.nn.log_sigmoid(-logits)
    miss = 1.0 - target
    miss = miss * miss
    pos_term = -(1.0 - prob) * (1.0 - prob) * log_p
    neg_term = -(miss * miss) * prob * prob * log_q
    return jnp.sum(jnp.where(positive, pos_term, neg_term)) / count


def select_cells(wide, offsets, sign, span, rows, cols, chans):

    def one_scene(field, offset):
        zero = jnp.zeros((), jnp.int32)
        start_r = span + sign * offset[0]
        start_c = span + sign * offset[1]
        return lax.dynamic_slice(field, (start_r, start_c, zero), (rows, cols, chans))

    return jax.vmap(one_scene)(wide, offsets)


def per_device(
    current, previous, offsets, center_rows, center_cols, classes, w_merge1, w_merge2, w_head
):
    scenes, rows, cols, chans = current.shape
    n_cls = w_head.shape[1]
    count = center_rows.shape[0] * center_rows.shape[1]
    span = min(rows, cols) * 3 // 4
    row_start = lax.axis_index("gx") * rows
    col_start = lax.axis_index("gy") * cols
    wide = extended(previous, (("gx", 1), ("gy", 2)), span)
    aligned = select_cells(wide, offsets, -1, span, rows, cols, chans)
    stacked = jnp.concatenate([current, aligned], axis=3)
    stack_ext = extended(stacked, (("gx", 1), ("gy", 2)), 1)
    pre1 = convolve(stack_ext, w_merge1, rows, cols)
    hidden1 = jax.nn.silu(pre1).astype(jnp.bfloat16).reshape(scenes, rows, cols, chans)
    hid_ext = extended(hidden1, (("gx", 1), ("gy", 2)), 1)
    pre2 = convolve(hid_ext, w_merge2, rows, cols)
    hidden2 = jax.nn.silu(pre2).astype(jnp.bfloat16)
    logits = (jnp.dot(hidden2, w_head, preferred_element_type=jnp.float32) - 2.19).reshape(
        scenes, rows, cols, n_cls
    )
    grid_row_ids = row_start + jnp.arange(rows, dtype=jnp.int32)
    grid_col_ids = col_start + jnp.arange(cols, dtype=jnp.int32)
    onehot = (classes[:, :, None] == jnp.arange(n_cls, dtype=jnp.int32)[None, None, :]).astype(
        jnp.float32
    )
    dr = (grid_row_ids[None, :, None] - center_rows[:, None, :]).astype(jnp.float32)
    dc = (grid_col_ids[None, :, None] - center_cols[:, None, :]).astype(jnp.float32)
    bump = jnp.exp(-(dr * dr)[:, :, None, :] / 8.0 - (dc * dc)[:, None, :, :] / 8.0)
    target = jnp.max(bump[..., None] * onehot[:, None, None, :, :], axis=3)
    hit = (
        (grid_row_ids[None, :, None] == center_rows[:, None, :])[:, :, None, :]
        & (grid_col_ids[None, :, None] == center_cols[:, None, :])[:, None, :, :]
    ).astype(jnp.float32)
    positive = jnp.einsum("srco,sok->srck", hit, onehot) > 0.5
    loss_part, back = jax.vjp(lambda z: focal(z, target, positive, count), logits)
    d_logits = back(jnp.ones((), jnp.float32))[0].astype(jnp.bfloat16).reshape(-1, n_cls)
    head_part = lax.dot_general(
        hidden2, d_logits, (((0,), (0,)), ((), ())), preferred_element_type=jnp.float32
    )
    d_hid2 = jnp.dot(d_logits, w_head.T, preferred_element_type=jnp.float32)
    d_pre2 = (d_hid2 * silu_grad(pre2)).astype(jnp.bfloat16)
    merge2_part = weight_grad(hid_ext, d_pre2, rows, cols)
    dpad2 = extended(d_pre2.reshape(scenes, rows, cols, chans), (("gx", 1), ("gy", 2)), 1)
    d_hid1 = back_convolve(dpad2, w_merge2, rows, cols)
    d_pre1 = (d_hid1 * silu_grad(pre1)).astype(jnp.bfloat16)
    merge1_part = weight_grad(stack_ext, d_pre1, rows, cols)
    dpad1 = extended(d_pre1.reshape(scenes, rows, cols, chans), (("gx", 1), ("gy", 2)), 1)
    d_stack = back_convolve(dpad1, w_merge1, rows, cols).reshape(scenes, rows, cols, 2 * chans)
    grad_current = d_stack[..., :chans].astype(jnp.bfloat16)
    d_aligned = d_stack[..., chans:].astype(jnp.bfloat16)
    back_wide = extended(d_aligned, (("gx", 1), ("gy", 2)), span)
    grad_previous = select_cells(back_wide, offsets, 1, span, rows, cols, chans)
    part = jnp.concatenate([
        merge1_part.reshape(-1, chans), merge2_part.reshape(-1, chans),
        jnp.pad(head_part.T, ((0, 16 - n_cls), (0, 0))),
        jnp.full((8, chans), loss_part, jnp.float32),
        jnp.zeros((ROWS - 3480, chans), jnp.float32)])
    total = all_reduce(part)
    merge1_total = total[:2304].reshape(3, 3, 2 * chans, chans)
    merge2_total = total[2304:3456].reshape(3, 3, chans, chans)
    head_total = total[3456 : 3456 + n_cls].T
    loss = total[3472, 0]
    return (loss, merge1_total, merge2_total, head_total, grad_current, grad_previous)


def solution(mesh):
    placed = (
        P(None, "gx", "gy", None),
        P(None, "gx", "gy", None),
        P(),
        P(),
        P(),
        P(),
        P(),
        P(),
        P(),
    )
    return jax.shard_map(
        per_device,
        mesh=mesh,
        in_specs=placed,
        out_specs=(P(), P(), P(), P(), P(None, "gx", "gy", None), P(None, "gx", "gy", None)),
        check_vma=False,
    )
```

```python
import jax
import jax.numpy as jnp
from jax import lax
from jax.experimental import pallas as pl
from jax.experimental.pallas import tpu as pltpu
from jax.sharding import PartitionSpec as P

FAR = 1e9
ROWS = 4096
HALF, QX, QY, QZ = ROWS // 2, ROWS // 8, ROWS // 32, ROWS // 512
MESH = pl.DeviceIdType.MESH


def place():
    gx, gy = lax.axis_index("gx"), lax.axis_index("gy")
    return gx % 2, gy % 4, (gx // 2) % 4, (gy // 4) * 4 + gx // 8


def device(core, x, y, z):
    return {"gx": ((z % 4) * 4 + y) * 2 + core, "gy": (z // 4) * 4 + x}
AROUND = tuple((r, c) for r in (-1, 0, 1) for c in (-1, 0, 1) if r or c)
VM = pl.BlockSpec(memory_space=pltpu.VMEM)


def around():
    gx, gy = lax.axis_index("gx"), lax.axis_index("gy")
    return [{"gx": (gx + r + 32) % 32, "gy": (gy + c + 16) % 16} for r, c in AROUND]


def exchange(src, dst, high, wide, send, recv, base):
    copies = []
    for n, ((r, c), peer) in enumerate(zip(AROUND, around())):
        r0, r1, nr = {1: (8 - high, 0, high), -1: (0, high + 8, high), 0: (0, high, 8)}[r]
        c0, c1, nc = {1: (8 - wide, 0, wide), -1: (0, wide + 8, wide), 0: (0, wide, 8)}[c]
        one = pltpu.make_async_remote_copy(
            src_ref=src.at[r0 : r0 + nr, c0 : c0 + nc], dst_ref=dst.at[r1 : r1 + nr, c1 : c1 + nc],
            send_sem=send.at[base + n], recv_sem=recv.at[base + n], device_id=peer, device_id_type=MESH,
        )
        one.start()
        copies.append(one)
    dst[high : high + 8, wide : wide + 8] = src[...]
    return copies


def greet():
    barrier = pltpu.get_barrier_semaphore()
    for peer in around():
        pl.semaphore_signal(barrier, inc=1, device_id=peer, device_id_type=MESH)
    pl.semaphore_wait(barrier, 8)


def inputs_kernel(cur_ref, prev_ref, obj_ref, cur_wide, prev_wide, near_ref, send, recv):
    greet()
    copies = exchange(prev_ref, prev_wide, 8, 4, send, recv, 0)
    copies += exchange(cur_ref, cur_wide, 2, 1, send, recv, 8)
    lane = lax.broadcasted_iota(jnp.int32, (1, 512), 1)
    scene = lane % 4
    row = (lane // 64 + lax.axis_index("gx") * 8).astype(jnp.float32)
    col = ((lane // 4) % 16 + lax.axis_index("gy") * 16).astype(jnp.float32)

    def of_scene(first):
        value = jnp.broadcast_to(obj_ref[:, first : first + 1], (64, 512))
        for s in range(1, 4):
            value = jnp.where(scene == s, obj_ref[:, first + s : first + s + 1], value)
        return value

    dr = row - of_scene(0)
    dc = col - of_scene(4)
    kind = of_scene(8)
    square = dr * dr + dc * dc
    for k in range(16):
        near_ref[k : k + 1] = jnp.min(jnp.where(kind == k, square, FAR), axis=0, keepdims=True)
    for one in copies:
        one.wait()


def exchange_inputs(cur, prev, obj):
    shape, D = jax.ShapeDtypeStruct, pltpu.SemaphoreType.DMA
    return pl.pallas_call(
        inputs_kernel,
        out_shape=(
            shape((12, 10, 8, 128), jnp.bfloat16), shape((24, 16, 8, 128), jnp.bfloat16),
            shape((16, 512), jnp.float32),
        ),
        in_specs=[VM] * 3, out_specs=(VM,) * 3,
        scratch_shapes=[D((16,)), D((16,))],
        compiler_params=pltpu.CompilerParams(collective_id=2, has_side_effects=True),
        name="exchange_inputs",
    )(cur, prev, obj)


def border_kernel(src_ref, dst_ref, send, recv):
    greet()
    for one in exchange(src_ref, dst_ref, 2, 1, send, recv, 0):
        one.wait()


def exchange_border(field):
    D = pltpu.SemaphoreType.DMA
    return pl.pallas_call(
        border_kernel,
        out_shape=jax.ShapeDtypeStruct((12, 10, 8, 128), jnp.bfloat16),
        in_specs=[VM], out_specs=VM,
        scratch_shapes=[D((8,)), D((8,))],
        compiler_params=pltpu.CompilerParams(collective_id=3, has_side_effects=True),
        name="exchange_border",
    )(field)


def reduce_kernel(
    g1_in, g2_in, misc_in, field_ref, g1_ref, g2_ref, misc_ref, wide_ref, part_ref,
    half_in, half, x_out, x_in, x_own, y_out, y_in, y_own, z_in, z_all,
    y_all, x_all, c_all, h_send, h_recv, c_send, c_recv, x_send, x_recv, y_send, y_recv, z_send, z_recv,
):
    core, x, y, z = place()
    partner = device(1 - core, x, y, z)
    xs = [device(core, (x + d) % 4, y, z) for d in range(1, 4)]
    ys = [device(core, x, (y + d) % 4, z) for d in range(1, 4)]
    zs = [device(core, x, y, (z + d) % 16) for d in range(1, 16)]
    barrier = pltpu.get_barrier_semaphore()
    for peer in [partner, *xs, *ys, *zs, *around()]:
        pl.semaphore_signal(barrier, inc=1, device_id=peer, device_id_type=MESH)
    pl.semaphore_wait(barrier, 30)
    part_ref[0:2304] = g1_in[...]
    part_ref[2304:3456] = g2_in[...]
    part_ref[3456:3480] = misc_in[...]
    part_ref[3480:ROWS] = jnp.zeros((ROWS - 3480, 128), jnp.float32)

    def copy(src, dst, send, recv, peer):
        one = pltpu.make_async_remote_copy(
            src_ref=src, dst_ref=dst, send_sem=send, recv_sem=recv,
            device_id=peer, device_id_type=MESH,
        )
        one.start()
        return one

    theirs = pl.multiple_of((1 - core) * HALF, HALF)
    mine = pl.multiple_of(core * HALF, HALF)
    c = copy(part_ref.at[pl.ds(theirs, HALF)], half_in, c_send.at[0], c_recv.at[0], partner)
    halo = exchange(field_ref, wide_ref, 6, 3, h_send, h_recv, 0)
    c.wait()
    total = part_ref[pl.ds(mine, HALF)] + half_in[...]
    half[...] = total
    x_out[...] = total.astype(jnp.bfloat16)
    cs = [
        copy(x_out.at[pl.ds(pl.multiple_of(((x + d) % 4) * QX, QX), QX)], x_in.at[d - 1],
             x_send.at[d - 1], x_recv.at[d - 1], xs[d - 1])
        for d in range(1, 4)
    ]
    total = half[pl.ds(pl.multiple_of(x * QX, QX), QX)]
    for d in range(3):
        cs[d].wait()
        total = total + x_in[d].astype(jnp.float32)
    x_own[...] = total
    y_out[...] = total.astype(jnp.bfloat16)
    cs = [
        copy(y_out.at[pl.ds(pl.multiple_of(((y + d) % 4) * QY, QY), QY)], y_in.at[d - 1],
             y_send.at[d - 1], y_recv.at[d - 1], ys[d - 1])
        for d in range(1, 4)
    ]
    total = x_own[pl.ds(pl.multiple_of(y * QY, QY), QY)]
    for d in range(3):
        cs[d].wait()
        total = total + y_in[d].astype(jnp.float32)
    y_own[...] = total
    cs = [
        copy(y_own.at[pl.ds(pl.multiple_of(((z + d) % 16) * QZ, QZ), QZ)], z_in.at[d - 1],
             z_send.at[d - 1], z_recv.at[d - 1], zs[d - 1])
        for d in range(1, 16)
    ]
    total = y_own[pl.ds(pl.multiple_of(z * QZ, QZ), QZ)]
    for d in range(15):
        cs[d].wait()
        total = total + z_in[d]
    own = pl.ds(pl.multiple_of(z * QZ, QZ), QZ)
    z_all[own] = total
    cs = [
        copy(z_all.at[own], z_all.at[own], z_send.at[14 + d], z_recv.at[14 + d], zs[d - 1])
        for d in range(1, 16)
    ]
    for one in cs:
        one.wait()
    own = pl.ds(pl.multiple_of(y * QY, QY), QY)
    y_all[own] = z_all[...].astype(jnp.bfloat16)
    cs = [
        copy(y_all.at[own], y_all.at[own], y_send.at[2 + d], y_recv.at[2 + d], ys[d - 1])
        for d in range(1, 4)
    ]
    for one in cs:
        one.wait()
    own = pl.ds(pl.multiple_of(x * QX, QX), QX)
    x_all[own] = y_all[...]
    cs = [
        copy(x_all.at[own], x_all.at[own], x_send.at[2 + d], x_recv.at[2 + d], xs[d - 1])
        for d in range(1, 4)
    ]
    for one in cs:
        one.wait()
    c = copy(x_all, c_all, c_send.at[1], c_recv.at[1], partner)
    for one in halo:
        one.wait()
    c.wait()
    first = core == 0
    low = jnp.where(first, x_all[...], c_all[...]).astype(jnp.float32)
    high = jnp.where(first, c_all[...], x_all[...]).astype(jnp.float32)
    g1_ref[0:HALF] = low
    g1_ref[HALF:2304] = high[0 : 2304 - HALF]
    g2_ref[...] = high[2304 - HALF : 3456 - HALF]
    misc_ref[...] = high[3456 - HALF : 3480 - HALF]


def all_reduce(g1, g2, misc, field):
    bf, f = jnp.bfloat16, jnp.float32
    V, D = pltpu.VMEM, pltpu.SemaphoreType.DMA
    shape = jax.ShapeDtypeStruct
    return pl.pallas_call(
        reduce_kernel,
        out_shape=(shape((2304, 128), f), shape((1152, 128), f), shape((24, 128), f), shape((20, 14, 8, 128), bf)),
        in_specs=[VM] * 4,
        out_specs=(VM,) * 4,
        scratch_shapes=[
            V((ROWS, 128), f),
            V((HALF, 128), f), V((HALF, 128), f), V((HALF, 128), bf), V((3, QX, 128), bf), V((QX, 128), f),
            V((QX, 128), bf), V((3, QY, 128), bf), V((QY, 128), f), V((15, QZ, 128), f), V((QY, 128), f),
            V((QX, 128), bf), V((HALF, 128), bf), V((HALF, 128), bf),
            D((8,)), D((8,)), D((2,)), D((2,)), D((6,)), D((6,)), D((6,)), D((6,)), D((30,)), D((30,)),
        ],
        compiler_params=pltpu.CompilerParams(collective_id=1, has_side_effects=True),
        name="all_reduce",
    )(g1, g2, misc, field)


def silu_grad(value, sig):
    return sig * (1.0 + value * (1.0 - sig))


def inside(shape, halo, width):
    row = lax.broadcasted_iota(jnp.int32, shape, 0) + (lax.axis_index("gx") * 8 - halo)
    lane = lax.broadcasted_iota(jnp.int32, shape, 1)
    col = lane // 4 + (lax.axis_index("gy") * 16 - halo)
    return (row >= 0) & (row < 256) & (col >= 0) & (col < 256) & (lane < width)


def dot(a, b, dims):
    return lax.dot_general(a, b, (dims, ((), ())), preferred_element_type=jnp.float32)


NN, NT, TN = ((1,), (0,)), ((1,), (1,)), ((0,), (0,))


def forward_kernel(
    st_ref, w1_ref, w2_ref, head_ref, near_ref,
    pre1_ref, patch1_ref, d2_ref, g2_ref, misc_ref, wide, hid, patch2,
):
    bf, f = jnp.bfloat16, jnp.float32
    wide[:, 0:80] = st_ref[...].astype(f)
    wide[:, 80:88] = jnp.zeros((12, 8, 256), f)
    for j in range(3):
        moved = wide[:, 4 * j : 4 * j + 80].astype(bf)
        for i in range(3):
            at = (3 * i + j) * 256
            patch1_ref[:, at : at + 256] = moved[i : i + 10].reshape(800, 256)
    pre1 = dot(patch1_ref[...], w1_ref[...], NN)
    pre1_ref[...] = pre1
    hidden = (pre1 * jax.nn.sigmoid(pre1)).astype(bf).astype(f).reshape(10, 80, 128)
    hid[...] = jnp.where(inside((10, 80, 128), 1, 72), hidden, 0.0)
    for j in range(3):
        moved = hid[:, 4 * j : 4 * j + 64].astype(bf)
        for i in range(3):
            at = (3 * i + j) * 128
            patch2[:, at : at + 128] = moved[i : i + 8].reshape(512, 128)
    pre2 = dot(patch2[...], w2_ref[...], NN)
    sig2 = jax.nn.sigmoid(pre2)
    hidden2 = (pre2 * sig2).astype(bf)
    z = dot(head_ref[...], hidden2, NT) - 2.19
    near = near_ref[...]
    real = lax.broadcasted_iota(jnp.int32, (16, 512), 0) < 10
    p = jax.nn.sigmoid(z)
    u = jnp.log1p(jnp.exp(-jnp.abs(z)))
    log_p = jnp.minimum(z, 0.0) - u
    log_q = jnp.minimum(-z, 0.0) - u
    q = 1.0 - p
    miss = 1.0 - jnp.where(near < FAR, jnp.exp(near * -0.125), 0.0)
    miss = miss * miss
    miss = miss * miss
    hit = near == 0.0
    loss = jnp.where(hit, -q * q * log_p, -miss * p * p * log_q)
    slope = jnp.where(hit, q * q * (2.0 * p * log_p - q), miss * p * p * (p - 2.0 * q * log_q))
    loss = jnp.where(real, loss, 0.0) * (1.0 / 256.0)
    slope = jnp.where(real, slope, 0.0) * (1.0 / 256.0)
    total = jnp.sum(jnp.sum(loss, axis=0, keepdims=True), axis=1, keepdims=True)
    d_z = slope.astype(bf)
    misc_ref[0:16] = dot(d_z, hidden2, NN)
    misc_ref[16:24] = jnp.broadcast_to(total, (8, 128))
    d_hid2 = dot(d_z, head_ref[...], TN)
    d2 = (d_hid2 * silu_grad(pre2, sig2)).astype(bf)
    d2_ref[...] = d2
    g2 = dot(d2, patch2[...], TN)
    for t in range(9):
        at = t * 128
        g2_ref[at : at + 128] = g2[:, at : at + 128].T


def forward(st, w1, w2, head, near):
    bf, f = jnp.bfloat16, jnp.float32
    shape, V = jax.ShapeDtypeStruct, pltpu.VMEM
    return pl.pallas_call(
        forward_kernel,
        out_shape=(
            shape((800, 128), f), shape((800, 2304), bf), shape((512, 128), bf), shape((1152, 128), f),
            shape((24, 128), f),
        ),
        in_specs=[VM] * 5, out_specs=(VM,) * 5,
        scratch_shapes=[V((12, 88, 256), f), V((10, 80, 128), f), V((512, 1152), bf)],
        name="forward",
    )(st, w1, w2, head, near)


def backward_kernel(
    d2_ref, pre1_ref, patch1_ref, w1_ref, w2_ref, g1_ref, cur_ref, al_ref, wide, wide1,
):
    bf, f = jnp.bfloat16, jnp.float32
    wide[:, 0:80] = jnp.where(inside((12, 80, 128), 2, 80), d2_ref[...].astype(f), 0.0)
    wide[:, 80:88] = jnp.zeros((12, 8, 128), f)
    d_hid1 = jnp.zeros((800, 128), f)
    for j in range(3):
        moved = wide[:, 8 - 4 * j : 88 - 4 * j].astype(bf)
        for i in range(3):
            at = (3 * i + j) * 128
            d_hid1 += dot(moved[2 - i : 12 - i].reshape(800, 128), w2_ref[at : at + 128], NT)
    pre1 = pre1_ref[...]
    d1 = d_hid1 * silu_grad(pre1, jax.nn.sigmoid(pre1))
    d1 = d1.astype(bf).astype(f).reshape(10, 80, 128)
    d1 = jnp.where(inside((10, 80, 128), 1, 72), d1, 0.0)
    wide1[...] = d1
    row = lax.broadcasted_iota(jnp.int32, (10, 80, 128), 0)
    lane = lax.broadcasted_iota(jnp.int32, (10, 80, 128), 1)
    tile = (row >= 1) & (row < 9) & (lane >= 4) & (lane < 68)
    own = jnp.where(tile, d1, 0.0).astype(bf).reshape(800, 128)
    g1 = dot(own, patch1_ref[...], TN)
    for t in range(18):
        at = t * 128
        g1_ref[at : at + 128] = g1[:, at : at + 128].T
    d_st = jnp.zeros((512, 256), f)
    for j in range(3):
        moved = wide1[:, 8 - 4 * j : 72 - 4 * j].astype(bf)
        for i in range(3):
            at = (3 * i + j) * 256
            d_st += dot(moved[2 - i : 10 - i].reshape(512, 128), w1_ref[at : at + 256], NT)
    cur_ref[...] = d_st[:, 0:128].astype(bf)
    al_ref[...] = d_st[:, 128:256].astype(bf)


def backward(d2, pre1, patch1, w1, w2):
    bf, f = jnp.bfloat16, jnp.float32
    shape, V = jax.ShapeDtypeStruct, pltpu.VMEM
    return pl.pallas_call(
        backward_kernel,
        out_shape=(shape((2304, 128), f), shape((512, 128), bf), shape((512, 128), bf)),
        in_specs=[VM] * 5, out_specs=(VM,) * 3,
        scratch_shapes=[V((12, 88, 128), f), V((10, 80, 128), f)],
        name="backward",
    )(d2, pre1, patch1, w1, w2)


def within(size, first, shift, limit):
    at = first + jnp.arange(size, dtype=jnp.int32)[:, None]
    return (at >= 0) & (at < limit) & (at + shift >= 0) & (at + shift < limit)


def slide(wide, rows, cols, starts):
    parts = [
        lax.dynamic_slice(wide[:, :, s], (starts[s, 0], starts[s, 1], jnp.int32(0)), (rows, cols, 128))
        for s in range(4)
    ]
    return jnp.stack(parts, axis=2)


def per_device(
    current, previous, offsets, center_rows, center_cols, classes, w_merge1, w_merge2, w_head
):
    bf = jnp.bfloat16
    row0, col0 = lax.axis_index("gx") * 8, lax.axis_index("gy") * 16
    n_cls = w_head.shape[1]
    cur = current.transpose(1, 2, 0, 3).reshape(8, 8, 8, 128)
    prev = previous.transpose(1, 2, 0, 3).reshape(8, 8, 8, 128)
    obj = jnp.concatenate([center_rows, center_cols, classes]).T.astype(jnp.float32)
    cur_wide, prev_wide, near = exchange_inputs(cur, prev, obj)
    zero = jnp.zeros((), bf)
    still = jnp.zeros((1, 4), jnp.int32)
    aligned = slide(prev_wide.reshape(24, 32, 4, 128), 12, 20, 6 - offsets)
    keep_rows = within(12, row0 - 2, -offsets[None, :, 0], 256)[:, None, :, None]
    keep_cols = within(20, col0 - 2, -offsets[None, :, 1], 256)[None, :, :, None]
    aligned = jnp.where(keep_rows & keep_cols, aligned, zero)
    on_rows = within(12, row0 - 2, still, 256)[:, None, :, None]
    on_cols = within(20, col0 - 2, still, 256)[None, :, :, None]
    near_cur = jnp.where(on_rows & on_cols, cur_wide.reshape(12, 20, 4, 128), zero)
    stacked = jnp.concatenate([near_cur, aligned], axis=3).reshape(12, 80, 256)
    w1, w2 = w_merge1.reshape(2304, 128), w_merge2.reshape(1152, 128)
    head = jnp.pad(w_head.T, ((0, 16 - n_cls), (0, 0)))
    pre1, patch1, d2, g2, misc = forward(stacked, w1, w2, head, near)
    d2 = exchange_border(d2.reshape(8, 8, 8, 128)).reshape(12, 80, 128)
    g1, g_cur, d_al = backward(d2, pre1, patch1, w1, w2)
    g1, g2, misc, back_wide = all_reduce(g1, g2, misc, d_al.reshape(8, 8, 8, 128))
    back = slide(back_wide.reshape(20, 28, 4, 128), 8, 16, 6 + offsets)
    keep_rows = within(8, row0, offsets[None, :, 0], 256)[:, None, :, None]
    keep_cols = within(16, col0, offsets[None, :, 1], 256)[None, :, :, None]
    grad_previous = jnp.where(keep_rows & keep_cols, back, zero).transpose(2, 0, 1, 3)
    grad_current = g_cur.reshape(8, 16, 4, 128).transpose(2, 0, 1, 3)
    return (
        misc[16, 0], g1.reshape(3, 3, 256, 128), g2.reshape(3, 3, 128, 128), misc[:n_cls].T,
        grad_current, grad_previous,
    )


def solution(mesh):
    placed = (
        P(None, "gx", "gy", None),
        P(None, "gx", "gy", None),
        P(),
        P(),
        P(),
        P(),
        P(),
        P(),
        P(),
    )
    return jax.shard_map(
        per_device,
        mesh=mesh,
        in_specs=placed,
        out_specs=(P(), P(), P(), P(), P(None, "gx", "gy", None), P(None, "gx", "gy", None)),
        check_vma=False,
    )
```
